256 devices in a mesh: expert: 32 (over z, x), tensor: 8 (over y, core).
Axes of the slice: x: 4, y: 4, z: 8, core: 2. Of those that a mesh axis runs over, the one named last changes fastest.
Arguments:
- attn_out: bfloat16 [4096, 4096], P('expert', 'tensor'), may hold values from -6 to 6
- residual: bfloat16 [4096, 4096], P('expert'), may hold values from -6 to 6
- o_weight: bfloat16 [4096, 4096], P('tensor'), may hold values from -0.09375 to 0.09375
- norm_gain: float32 [4096], replicated, may hold values from 0.5 to 1.5
- router_weight: bfloat16 [4096, 32], replicated, may hold values from -0.09375 to 0.09375
- expert_idx: int32 [4096, 8], P('expert'), may hold values from 0 to 31, all different within a row; in each aligned block of 16 rows (0 to 15, 16 to 31, ...) at most 6 rows name the same one
- combine: float32 [4096, 8], P('expert'), may hold values from 0.05 to 0.25
- w_gate: bfloat16 [32, 4096, 1536], P('expert', None, 'tensor'), may hold values from -0.09375 to 0.09375
- w_up: bfloat16 [32, 4096, 1536], P('expert', None, 'tensor'), may hold values from -0.09375 to 0.09375
- w_down: bfloat16 [32, 1536, 4096], P('expert', 'tensor'), may hold values from -0.15625 to 0.15625
Outputs:
- mixed: bfloat16 [4096, 4096], P('expert')
- router_logits: float32 [4096, 32], P('expert')
The draws below stay inside these ranges and needn't reach their ends.
Inputs may be any that keep to these rules, and one draw needn't show every extreme that they name: `expert_idx`: each row names 8 different experts. In each aligned block of 16 tokens no expert is named by more than 6 tokens, a bound that some block reaches.
All inputs are finite; a program needn't handle non-finite values.
Results may differ from the reference program's by a relative error of at most 0.015.
Values may be sent and summed in bfloat16 or wider, within the bound.
No kernel may reach another device: no remote copies, remote signals or barrier semaphores. Data moves between devices by JAX's collectives and lax.ppermute only.
A program may use at most 128 MiB of HBM per device.

```python
import math
import jax
import jax.numpy as jnp
import numpy as np
from jax import lax

D = 4096
HQ = 32
HD = 128
FF = 1536
TOP = 8
TOKENS = 4096
EXPERTS = 32
ROWS = 16
CAP = 6
N_TENSOR = 8


def level_of(rng, extent, shards, low, top_value):
    loudness = 1.0
    for axis_at, blocks in shards:
        draws = jax.random.uniform(jax.random.fold_in(jax.random.fold_in(rng, 6), axis_at), (blocks,), jnp.float32, low / len(shards), top_value / len(shards))
        loudness = loudness * jnp.repeat(jnp.exp(draws), extent[axis_at] // blocks).reshape((-1,) + (1,) * (len(extent) - 1 - axis_at))
    return loudness


def deal_out(rng, own, number, rows, amount, top, most, lean):
    sequence = jax.random.permutation(rng, amount)
    crowded, common = load_shares(amount, rows * top, most, lean, True), load_shares(amount, rows * top, most, lean, False)
    places = jnp.arange(amount)

    def named(lengths, offset_by):
        used = int((lengths > 0).sum())
        fixed = max(1, used // 4)
        shifted = fixed + (places - fixed + offset_by * (used - fixed)) % max(1, amount - fixed)
        return jnp.zeros((amount,), jnp.int32).at[sequence[jnp.where(places < fixed, places, shifted)]].set(jnp.asarray(lengths, jnp.int32))

    lengths = jnp.where(number % 4 == 0, named(crowded, number // 4), named(common, number - number // 4 - 1))
    mixed = jax.random.permutation(jax.random.fold_in(own, 3), amount)
    source_of, sink = mixed[0:amount // 2 * 2:2], mixed[1:amount // 2 * 2:2]
    margin = jnp.minimum(lengths[source_of] - 1, most - lengths[sink]) // 2
    margin = jnp.where((source_of == sequence[0]) | (sink == sequence[0]) | (lengths[sink] == 0), 0, jnp.maximum(margin, 0))
    shifted = jax.random.randint(jax.random.fold_in(own, 4), (amount // 2,), 0, 1 << 20) % (margin + 1)
    lengths = lengths.at[source_of].add(-shifted).at[sink].add(shifted)
    labels = jnp.searchsorted(jnp.cumsum(lengths), jnp.arange(rows * top), side="right").astype(jnp.int32)
    table = labels.reshape(top, rows).T
    table = table[jax.random.permutation(jax.random.fold_in(own, 1), rows)]
    offset_by = jax.random.randint(jax.random.fold_in(own, 2), (rows, 1), 0, top)
    return jnp.take_along_axis(table, (jnp.arange(top)[None, :] + offset_by) % top, axis=1)


def load_shares(amount, total, limit, slope, full):
    weights = [(1 << 20) // math.isqrt(standing ** slope) + 1 for standing in range(1, amount + 1)]
    largest = limit if full else min(limit, max(-(-total // amount), total * weights[0] // sum(weights)))
    least = 1 if total - largest >= amount - 1 else 0
    holding, spare = [largest] + [least] * (amount - 1), total - largest - least * (amount - 1)
    while spare > 0:
        candidates = [i for i in range(1, amount) if holding[i] < largest] or [i for i in range(1, amount) if holding[i] < limit]
        mass, left = sum([weights[i] for i in candidates]), spare
        for i in candidates:
            more = min(limit - holding[i], max(1, left * weights[i] // mass), spare)
            holding[i] = holding[i] + more
            spare = spare - more
    return np.array(holding)


def noise(rng, dims, scale, bound, cuts=(), kind=jnp.bfloat16):
    entries = scale * jax.random.normal(rng, dims, jnp.float32)
    if cuts:
        entries = entries * level_of(rng, dims, cuts, -0.22, 0.18)
    return jnp.clip(entries, -bound, bound).astype(kind)


def setup_inputs(seed: int = 0) -> dict:
    keys = jax.random.split(jax.random.key(seed), 11)
    attn_out = noise(keys[0], (TOKENS, HQ * HD), 1.0, 6.0, ((0, 32), (1, 8)))
    residual = noise(keys[1], (TOKENS, D), 1.0, 6.0, ((0, 32),))
    o_weight = noise(keys[2], (HQ * HD, D), (HQ * HD) ** -0.5, 0.09375, ((0, 8),))
    norm_gain = jnp.clip(1.0 + 0.1 * jax.random.normal(keys[3], (D,), jnp.float32), 0.5, 1.5)
    router_weight = noise(keys[4], (D, EXPERTS), D ** -0.5, 0.09375)
    expert_idx_keys = jax.random.split(jax.random.fold_in(keys[5], 1), TOKENS // ROWS)
    expert_idx_turns = jax.random.permutation(jax.random.fold_in(keys[5], 3), TOKENS // ROWS)
    expert_idx = jax.vmap(lambda own, number: deal_out(jax.random.fold_in(keys[5], 2), own, number, ROWS, EXPERTS, TOP, CAP, 2))(expert_idx_keys, expert_idx_turns).reshape((TOKENS, TOP))
    combine = jnp.clip(0.05 + 0.2 * jax.random.uniform(keys[6], (TOKENS, TOP), jnp.float32) ** level_of(keys[6], (TOKENS, TOP), ((0, 32),), -0.2, 0.2), 0.05, 0.25)
    w_gate = noise(keys[7], (EXPERTS, D, FF), D ** -0.5, 0.09375, ((0, 32), (2, 8)))
    w_up = noise(keys[8], (EXPERTS, D, FF), D ** -0.5, 0.09375, ((0, 32), (2, 8)))
    w_down = noise(keys[9], (EXPERTS, FF, D), FF ** -0.5, 0.15625, ((0, 32), (1, 8)))
    return {"attn_out": attn_out, "residual": residual, "o_weight": o_weight, "norm_gain": norm_gain, "router_weight": router_weight, "expert_idx": expert_idx, "combine": combine, "w_gate": w_gate, "w_up": w_up, "w_down": w_down}


epsilon = 1e-06

def reference(attn_out, residual, o_weight, norm_gain, router_weight, expert_idx, combine, w_gate, w_up, w_down):
    projected = jnp.dot(attn_out, o_weight, preferred_element_type=jnp.float32)
    stream = (residual.astype(jnp.float32) + projected).astype(jnp.bfloat16)
    stream_wide = stream.astype(jnp.float32)
    scale = lax.rsqrt(lax.optimization_barrier(jnp.mean(stream_wide * stream_wide, axis=-1, keepdims=True)) + epsilon)
    normed = (stream_wide * scale * norm_gain.astype(jnp.float32)).astype(jnp.bfloat16)
    router_logits = jnp.dot(normed, router_weight, preferred_element_type=jnp.float32)
    block_count = TOKENS // ROWS
    flat_ids = expert_idx.reshape(block_count, ROWS * TOP)
    one_hot = (flat_ids[:, :, None] == jnp.arange(EXPERTS, dtype=jnp.int32)[None, None, :]).astype(jnp.int32)
    slot_index = lax.optimization_barrier(jnp.sum((jnp.cumsum(one_hot, axis=1) - 1) * one_hot, axis=2)).astype(jnp.int32)
    block_ids = jnp.broadcast_to(jnp.arange(block_count, dtype=jnp.int32)[:, None], (block_count, ROWS * TOP))
    token_rows = jnp.repeat(jnp.arange(TOKENS, dtype=jnp.int32), TOP)
    expert_in = jnp.zeros((EXPERTS, block_count, CAP, D), jnp.bfloat16)
    expert_in = expert_in.at[flat_ids.reshape(-1), block_ids.reshape(-1), slot_index.reshape(-1)].set(normed[token_rows])

    def one_expert(operands):
        rows_in, gate_w, up_w, down_w = operands
        flat_rows = rows_in.reshape(block_count * CAP, D)
        gate = jnp.dot(flat_rows, gate_w, preferred_element_type=jnp.float32)
        up_val = jnp.dot(flat_rows, up_w, preferred_element_type=jnp.float32)
        hidden = (jax.nn.silu(gate) * up_val).astype(jnp.bfloat16)
        grouped = hidden.reshape(block_count * CAP, N_TENSOR, FF // N_TENSOR).astype(jnp.float32)
        down_grouped = down_w.reshape(N_TENSOR, FF // N_TENSOR, D).astype(jnp.float32)
        partials = jnp.einsum('sgf,gfd->gsd', grouped, down_grouped).astype(jnp.bfloat16)
        total = lax.optimization_barrier(jnp.sum(partials.astype(jnp.float32), axis=0)).astype(jnp.bfloat16)
        return total.reshape(block_count, CAP, D)
    expert_out = lax.map(one_expert, (expert_in, w_gate, w_up, w_down))
    token_block = (jnp.arange(TOKENS, dtype=jnp.int32) // ROWS)[:, None]
    picked = expert_out[expert_idx, jnp.broadcast_to(token_block, (TOKENS, TOP)), slot_index.reshape(TOKENS, TOP)]
    moe = lax.optimization_barrier(jnp.sum(combine[:, :, None] * picked.astype(jnp.float32), axis=1))
    mixed = (stream.astype(jnp.float32) + moe).astype(jnp.bfloat16)
    return (mixed, router_logits)
```

```python
import jax
import jax.numpy as jnp
from jax import lax
from jax.experimental import pallas as pl
from jax.experimental.pallas import tpu as pltpu
from jax.sharding import PartitionSpec as P


epsilon = 1e-06
PIECES = 8
f32 = jnp.float32
bf16 = jnp.bfloat16


def slot_targets(chosen, expert_count, capacity):
    flat_ids = chosen.reshape(-1)
    one_hot = (flat_ids[:, None] == jnp.arange(expert_count, dtype=jnp.int32)[None, :]).astype(
        jnp.int32
    )
    slot_index = jnp.sum((jnp.cumsum(one_hot, axis=0) - 1) * one_hot, axis=1)
    return (flat_ids * capacity + slot_index).reshape(chosen.shape)


def swap_matrix(capacity):
    size = PIECES * PIECES * capacity
    row = lax.broadcasted_iota(jnp.int32, (size, size), 0)
    col = lax.broadcasted_iota(jnp.int32, (size, size), 1)
    stride = PIECES * capacity
    source = (row % stride) // capacity * stride + row // stride * capacity + row % capacity
    return (col == source).astype(bf16)


def pieces_to_rows(x):
    width = x.shape[1] // PIECES
    return jnp.concatenate([x[:, j * width : (j + 1) * width] for j in range(PIECES)], axis=0)


def front_kernel(parts, residual, gain, router, hits, outbox, stream_out, logits_out):
    total = parts[0].astype(f32)
    for i in range(1, parts.shape[0]):
        total = total + parts[i].astype(f32)
    stream = (residual[...].astype(f32) + total).astype(bf16)
    wide = stream.astype(f32)
    scale = lax.rsqrt(jnp.mean(wide * wide, axis=-1, keepdims=True) + epsilon)
    normed = (wide * scale * gain[...]).astype(bf16)
    stream_out[...] = pieces_to_rows(stream)
    logits_out[...] = lax.dot_general(
        normed, router[...], (((1,), (1,)), ((), ())), preferred_element_type=f32
    )
    outbox[...] = lax.dot_general(
        hits[...],
        pieces_to_rows(normed),
        (((0,), (0,)), ((), ())),
        preferred_element_type=f32,
    ).astype(bf16)


def front(parts, residual, gain, router, hits):
    _, rows, width = parts.shape
    piece = width // PIECES
    return pl.pallas_call(
        front_kernel,
        out_shape=(
            jax.ShapeDtypeStruct((hits.shape[1], piece), bf16),
            jax.ShapeDtypeStruct((rows * PIECES, piece), bf16),
            jax.ShapeDtypeStruct((rows, router.shape[0]), f32),
        ),
        compiler_params=pltpu.CompilerParams(vmem_limit_bytes=40 * 2**20),
        name="front",
    )(parts, residual, gain, router, hits)


def swap_kernel(x, swap, out):
    moved = jnp.dot(swap[...], x[...], preferred_element_type=f32).astype(bf16)
    out[...] = moved.reshape(out.shape)


def rows_by_piece(x, swap):
    size = swap.shape[0]
    steps = x.shape[0] // size
    width = x.shape[1]
    run = size // PIECES
    return pl.pallas_call(
        swap_kernel,
        grid=(steps,),
        in_specs=[
            pl.BlockSpec((size, width), lambda a: (a, 0)),
            pl.BlockSpec((size, size), lambda a: (0, 0)),
        ],
        out_specs=pl.BlockSpec((PIECES, run, width), lambda a: (0, a, 0)),
        out_shape=jax.ShapeDtypeStruct((PIECES, run * steps, width), bf16),
        name="rows_by_piece",
    )(x, swap)


def dot_last(a, b):
    return lax.dot_general(a, b, (((1,), (1,)), ((), ())), preferred_element_type=f32)


def up_kernel(x, w_gate, w_up, out):
    width = x.shape[3]
    gate = None
    for j in range(PIECES):
        part = x[0, j]
        columns = slice(j * width, (j + 1) * width)
        g = dot_last(part, w_gate[:, columns])
        u = dot_last(part, w_up[:, columns])
        gate, up = (g, u) if gate is None else (gate + g, up + u)
    out[0] = (gate / (1.0 + jnp.exp(-gate)) * up).astype(bf16)


def up_rows(x, w_gate, w_up):
    ranks, pieces, rows, width = x.shape
    units, depth = w_gate.shape
    return pl.pallas_call(
        up_kernel,
        grid=(ranks,),
        in_specs=[
            pl.BlockSpec((1, pieces, rows, width), lambda r: (r, 0, 0, 0)),
            pl.BlockSpec((units, depth), lambda r: (0, 0)),
            pl.BlockSpec((units, depth), lambda r: (0, 0)),
        ],
        out_specs=pl.BlockSpec((1, rows, units), lambda r: (r, 0, 0)),
        out_shape=jax.ShapeDtypeStruct((ranks, rows, units), bf16),
        compiler_params=pltpu.CompilerParams(vmem_limit_bytes=40 * 2**20),
        name="up_rows",
    )(x, w_gate, w_up)


def down_kernel(hidden, w_down, swap, out, held):
    j = pl.program_id(0)
    ranks, rows, units = hidden.shape
    total = None
    for r in range(ranks):
        part = jnp.dot(
            hidden[r], w_down[r * units : (r + 1) * units, :], preferred_element_type=f32
        )
        total = part if total is None else total + part
    held[j] = total.astype(bf16)

    @pl.when(j == PIECES - 1)
    def _():
        size = swap.shape[0]
        run = size // PIECES
        for a in range(rows // run):
            block = held[:, a * run : (a + 1) * run, :].reshape(size, held.shape[2])
            out[a * size : (a + 1) * size, :] = jnp.dot(
                swap[...], block, preferred_element_type=f32
            ).astype(bf16)


def down_rows(hidden, w_down, swap):
    ranks, rows, units = hidden.shape
    depth, width = w_down.shape
    piece = width // PIECES
    return pl.pallas_call(
        down_kernel,
        grid=(PIECES,),
        in_specs=[
            pl.BlockSpec((ranks, rows, units), lambda j: (0, 0, 0)),
            pl.BlockSpec((depth, piece), lambda j: (0, j)),
            pl.BlockSpec(swap.shape, lambda j: (0, 0)),
        ],
        out_specs=pl.BlockSpec((rows * PIECES, piece), lambda j: (0, 0)),
        out_shape=jax.ShapeDtypeStruct((rows * PIECES, piece), bf16),
        scratch_shapes=[pltpu.VMEM((PIECES, rows, piece), bf16)],
        compiler_params=pltpu.CompilerParams(vmem_limit_bytes=40 * 2**20),
        name="down_rows",
    )(hidden, w_down, swap)


def finish_kernel(returned, weights, stream, logits, out):
    high = weights[...].astype(bf16)
    low = (weights[...] - high.astype(f32)).astype(bf16)
    moe = jnp.dot(high, returned[...], preferred_element_type=f32) + jnp.dot(
        low, returned[...], preferred_element_type=f32
    )
    rows = stream.shape[0]
    out[0:rows, :] = (stream[...].astype(f32) + moe).astype(bf16)
    logit_high = logits[...].astype(bf16)
    logit_low = (logits[...] - logit_high.astype(f32)).astype(bf16)
    count = logits.shape[1]
    filler = jnp.zeros((logits.shape[0], out.shape[1] - 2 * count), bf16)
    out[rows:, :] = jnp.concatenate([logit_high, logit_low, filler], axis=1)


def finish(returned, weights, stream, logits):
    return pl.pallas_call(
        finish_kernel,
        out_shape=jax.ShapeDtypeStruct(
            (stream.shape[0] + logits.shape[0], stream.shape[1]), bf16
        ),
        compiler_params=pltpu.CompilerParams(vmem_limit_bytes=40 * 2**20),
        name="finish",
    )(returned, weights, stream, logits)


def routing(chosen, combine, expert_count, capacity):
    targets = slot_targets(chosen, expert_count, capacity)
    tokens = chosen.shape[0]
    total = expert_count * PIECES * capacity
    row = lax.broadcasted_iota(jnp.int32, (PIECES * tokens, total), 0)
    col = lax.broadcasted_iota(jnp.int32, (PIECES * tokens, total), 1)
    run = PIECES * capacity
    same_piece = row // tokens == (col % run) // capacity
    slot_of = col // run * capacity + col % capacity
    wanted = jnp.where(same_piece, slot_of, -1)
    targets = jnp.tile(targets, (PIECES, 1))
    combine = jnp.tile(combine, (PIECES, 1))
    weights = jnp.zeros((PIECES * tokens, total), f32)
    hits = jnp.zeros((PIECES * tokens, total), jnp.bool_)
    for k in range(chosen.shape[1]):
        match = wanted == targets[:, k : k + 1]
        weights = weights + jnp.where(match, combine[:, k : k + 1], 0.0)
        hits = hits | match
    return hits.astype(bf16), weights


def shards(
    attn_out,
    residual,
    o_weight,
    norm_gain,
    router_weight,
    expert_idx,
    combine,
    w_gate,
    w_up,
    w_down,
):
    ranks = lax.axis_size("tensor")
    rank = lax.axis_index("tensor")
    group_rows, width = residual.shape
    rows = group_rows // ranks
    piece = width // PIECES
    expert_count = router_weight.shape[1]
    top_count = expert_idx.shape[1]
    capacity = min(rows, max(2, 3 * rows * top_count // (2 * expert_count)))

    w_down_all = lax.all_gather(w_down[0], "tensor", axis=0, tiled=True)
    swap = swap_matrix(capacity)
    chosen = lax.dynamic_slice_in_dim(expert_idx, rank * rows, rows, 0)
    my_combine = lax.dynamic_slice_in_dim(combine, rank * rows, rows, 0)
    hits, weights = routing(chosen, my_combine, expert_count, capacity)
    my_residual = lax.dynamic_slice_in_dim(residual, rank * rows, rows, 0)

    partial = jnp.dot(attn_out, o_weight, preferred_element_type=f32).astype(bf16)
    parts = lax.all_to_all(partial, "tensor", split_axis=0, concat_axis=0, tiled=True)
    outbox, stream, logits = front(
        parts.reshape(ranks, rows, width),
        my_residual,
        norm_gain.reshape(1, width),
        router_weight.T,
        hits,
    )
    arrived = lax.all_to_all(outbox, "expert", split_axis=0, concat_axis=0, tiled=True)
    by_piece = rows_by_piece(arrived, swap)
    everyone = lax.all_gather(by_piece, "tensor", axis=0, tiled=False)
    hidden = up_rows(everyone, w_gate[0].T, w_up[0].T)
    my_hidden = lax.all_to_all(hidden, "tensor", split_axis=0, concat_axis=0, tiled=True)
    expert_out = down_rows(my_hidden, w_down_all, swap)
    returned = lax.all_to_all(expert_out, "expert", split_axis=0, concat_axis=0, tiled=True)
    packed = finish(returned, weights, stream, logits)
    gathered = lax.all_gather(packed, "tensor", axis=0, tiled=False)
    mixed = (
        gathered[:, : PIECES * rows]
        .reshape(ranks, PIECES, rows, piece)
        .transpose(0, 2, 1, 3)
        .reshape(group_rows, width)
    )
    tail = gathered[:, PIECES * rows :].astype(f32)
    logits_group = (tail[:, :, :expert_count] + tail[:, :, expert_count : 2 * expert_count]).reshape(
        group_rows, expert_count
    )
    return mixed, logits_group


def solution(mesh):
    in_specs = (
        P("expert", "tensor"),
        P("expert", None),
        P("tensor", None),
        P(),
        P(),
        P("expert", None),
        P("expert", None),
        P("expert", None, "tensor"),
        P("expert", None, "tensor"),
        P("expert", "tensor", None),
    )
    out_specs = (P("expert", None), P("expert", None))

    return jax.shard_map(shards, mesh=mesh, in_specs=in_specs, out_specs=out_specs, check_vma=False)
```

```python
import jax
import jax.numpy as jnp
from jax import lax
from jax.experimental import pallas as pl
from jax.experimental.pallas import tpu as pltpu
from jax.sharding import PartitionSpec as P


epsilon = 1e-06
PIECES = 8
HALVES = 2
CHIPS = 4
BATCH = 16
f32 = jnp.float32
bf16 = jnp.bfloat16
roomy = pltpu.CompilerParams(vmem_limit_bytes=44 * 2**20)


def slot_targets(chosen, expert_count, capacity):
    flat_ids = chosen.reshape(-1)
    one_hot = (flat_ids[:, None] == jnp.arange(expert_count, dtype=jnp.int32)[None, :]).astype(
        jnp.int32
    )
    slot_index = jnp.sum((jnp.cumsum(one_hot, axis=0) - 1) * one_hot, axis=1)
    return (flat_ids * capacity + slot_index).reshape(chosen.shape)


def reorder_matrix(outer, inner, run):
    size = outer * inner * run
    row = lax.broadcasted_iota(jnp.int32, (size, size), 0)
    col = lax.broadcasted_iota(jnp.int32, (size, size), 1)
    a = row // (inner * run)
    b = row % (inner * run) // run
    return (col == b * (outer * run) + a * run + row % run).astype(bf16)


def pieces_to_rows(x):
    width = x.shape[1] // PIECES
    return jnp.concatenate([x[:, j * width : (j + 1) * width] for j in range(PIECES)], axis=0)


def dot_last(a, b):
    return lax.dot_general(a, b, (((1,), (1,)), ((), ())), preferred_element_type=f32)


def dot_first(a, b):
    return lax.dot_general(a, b, (((0,), (0,)), ((), ())), preferred_element_type=f32)


def along(x, shift):
    pairs = [
        (2 * chip + core, 2 * ((chip + shift) % CHIPS) + core)
        for chip in range(CHIPS)
        for core in range(2)
    ]
    return lax.ppermute(x, "tensor", pairs)


def across(x):
    return lax.ppermute(x, "tensor", [(r, r ^ 1) for r in range(2 * CHIPS)])


def project_kernel(place, attn, weight, mine, theirs):
    rows = mine.shape[1]
    chip, core = place[0], place[1]

    def block(shift, other):
        rank = 2 * ((chip + shift) % CHIPS) + (core + other) % 2
        return attn[pl.ds(pl.multiple_of(rank * rows, rows), rows), :]

    ordered = [block(shift, other) for other in range(2) for shift in range(CHIPS)]
    total = jnp.dot(
        jnp.concatenate(ordered, axis=0), weight[...], preferred_element_type=f32
    ).astype(bf16)
    for i in range(CHIPS):
        mine[i] = total[i * rows : (i + 1) * rows, :]
        theirs[i] = total[(CHIPS + i) * rows : (CHIPS + i + 1) * rows, :]


def project(place, attn, weight):
    depth, width = weight.shape
    rows = attn.shape[0] // (2 * CHIPS)
    step = width // 4
    out = jax.ShapeDtypeStruct((CHIPS, rows, width), bf16)
    return pl.pallas_call(
        project_kernel,
        grid_spec=pltpu.PrefetchScalarGridSpec(
            num_scalar_prefetch=1,
            grid=(4,),
            in_specs=[
                pl.BlockSpec(attn.shape, lambda n, place: (0, 0)),
                pl.BlockSpec((depth, step), lambda n, place: (0, n)),
            ],
            out_specs=[pl.BlockSpec((CHIPS, rows, step), lambda n, place: (0, 0, n))] * 2,
        ),
        out_shape=(out, out),
        compiler_params=roomy,
        name="project",
    )(place, attn, weight)


def pair_kernel(mine, other, *outs):
    for i in range(CHIPS):
        outs[i][...] = (mine[i].astype(f32) + other[i].astype(f32)).astype(bf16)


def pair_sums(mine, other):
    out = jax.ShapeDtypeStruct(mine.shape[1:], bf16)
    return pl.pallas_call(
        pair_kernel, out_shape=(out,) * CHIPS, compiler_params=roomy, name="pair_sums"
    )(mine, other)


def front_kernel(place, p0, p1, p2, p3, residual, gain, router, shares0, shares1, *outs):
    outbox0, outbox1, stream_out, logits_out = outs
    rows = p0.shape[0]
    start = (2 * place[0] + place[1]) * rows
    total = (p0[...].astype(f32) + p1[...].astype(f32)) + (
        p2[...].astype(f32) + p3[...].astype(f32)
    )
    mine = residual[pl.ds(pl.multiple_of(start, rows), rows), :]
    stream = (mine.astype(f32) + total).astype(bf16)
    wide = stream.astype(f32)
    scale = lax.rsqrt(jnp.mean(wide * wide, axis=-1, keepdims=True) + epsilon)
    normed = (wide * scale * gain[...]).astype(bf16)
    stream_out[...] = pieces_to_rows(stream)
    logits_out[...] = dot_last(normed, router[...])
    by_piece = pieces_to_rows(normed)
    for shares, outbox in ((shares0, outbox0), (shares1, outbox1)):
        hits = (shares[...] != 0.0).astype(bf16)
        outbox[...] = dot_first(hits, by_piece).astype(bf16)


def front(place, parts, residual, gain, router, shares):
    rows, width = parts[0].shape
    piece = width // PIECES
    whole = pl.BlockSpec(memory_space=pltpu.VMEM)
    outbox = jax.ShapeDtypeStruct((shares[0].shape[1], piece), bf16)
    return pl.pallas_call(
        front_kernel,
        in_specs=[pl.BlockSpec(memory_space=pltpu.SMEM)] + [whole] * 9,
        out_shape=(
            outbox,
            outbox,
            jax.ShapeDtypeStruct((rows * PIECES, piece), bf16),
            jax.ShapeDtypeStruct((rows, router.shape[0]), f32),
        ),
        compiler_params=roomy,
        name="front",
    )(place, *parts, residual, gain, router, *shares)


def by_piece_kernel(x, order, low, high):
    moved = jnp.dot(order[...], x[...], preferred_element_type=f32)
    moved = moved.reshape((PIECES,) + low.shape[1:]).astype(bf16)
    low[...] = moved[: PIECES // 2]
    high[...] = moved[PIECES // 2 :]


def rows_by_piece(x, order):
    size = order.shape[0]
    steps = x.shape[0] // size
    width = x.shape[1]
    run = size // PIECES
    out = jax.ShapeDtypeStruct((PIECES // 2, run * steps, width), bf16)
    return pl.pallas_call(
        by_piece_kernel,
        grid=(steps,),
        in_specs=[
            pl.BlockSpec((size, width), lambda a: (a, 0)),
            pl.BlockSpec((size, size), lambda a: (0, 0)),
        ],
        out_specs=[pl.BlockSpec((PIECES // 2, run, width), lambda a: (0, a, 0))] * 2,
        out_shape=(out, out),
        name="rows_by_piece",
    )(x, order)


def up_kernel(*refs):
    lows, highs = refs[:CHIPS], refs[CHIPS : 2 * CHIPS]
    gate_own, gate_other, up_own, up_other = refs[2 * CHIPS : 2 * CHIPS + 4]
    outs = refs[2 * CHIPS + 5 : 3 * CHIPS + 5]
    gate, up = refs[3 * CHIPS + 5 :]
    j = pl.program_id(0)

    @pl.when(j == 0)
    def _():
        gate[...] = jnp.zeros_like(gate)
        up[...] = jnp.zeros_like(up)

    x = jnp.concatenate(
        [jnp.where(j < PIECES // 2, low[0], high[0]) for low, high in zip(lows, highs)], axis=0
    )
    gate[...] += dot_last(x, jnp.concatenate([gate_own[...], gate_other[...]], axis=0))
    up[...] += dot_last(x, jnp.concatenate([up_own[...], up_other[...]], axis=0))

    @pl.when(j == PIECES - 1)
    def _():
        g = gate[...]
        hidden = (g / (1.0 + jnp.exp(-g)) * up[...]).astype(bf16)
        rows = outs[0].shape[0]
        for i in range(CHIPS):
            outs[i][...] = hidden[i * rows : (i + 1) * rows, :]


def up_rows(lows, highs, weights, after):
    _, rows, width = lows[0].shape
    units = weights[0].shape[0]
    out = jax.ShapeDtypeStruct((rows, 2 * units), bf16)
    return pl.pallas_call(
        up_kernel,
        grid=(PIECES,),
        in_specs=[
            pl.BlockSpec((1, rows, width), lambda j: (jnp.minimum(j, PIECES // 2 - 1), 0, 0))
        ]
        * CHIPS
        + [pl.BlockSpec((1, rows, width), lambda j: (jnp.maximum(j - PIECES // 2, 0), 0, 0))]
        * CHIPS
        + [pl.BlockSpec((units, width), lambda j: (0, j))] * 4
        + [pl.BlockSpec(memory_space=pl.ANY)],
        out_specs=[pl.BlockSpec((rows, 2 * units), lambda j: (0, 0))] * CHIPS,
        out_shape=(out,) * CHIPS,
        scratch_shapes=[pltpu.VMEM((CHIPS * rows, 2 * units), f32)] * 2,
        compiler_params=roomy,
        name="up_rows",
    )(*lows, *highs, *weights, after)


def down_kernel(place, h0, h1, h2, h3, w_down, order, out, held):
    j = pl.program_id(0)
    chip, core = place[0], place[1]
    total = None
    for i, hidden in enumerate((h0, h1, h2, h3)):
        first = 2 * ((chip + i) % CHIPS)
        weight = jnp.concatenate([w_down[first + core], w_down[first + (core + 1) % 2]], axis=0)
        part = jnp.dot(hidden[...], weight, preferred_element_type=f32)
        total = part if total is None else total + part
    held[j] = total.astype(bf16)

    @pl.when(j == PIECES - 1)
    def _():
        size = order.shape[0]
        run = size // PIECES
        for a in range(held.shape[1] // run):
            block = held[:, a * run : (a + 1) * run, :].reshape(size, held.shape[2])
            out[a * size : (a + 1) * size, :] = dot_first(order[...], block).astype(bf16)


def down_rows(place, hidden, w_down, order):
    rows, units = hidden[0].shape
    ranks, depth, width = w_down.shape
    piece = width // PIECES
    return pl.pallas_call(
        down_kernel,
        grid_spec=pltpu.PrefetchScalarGridSpec(
            num_scalar_prefetch=1,
            grid=(PIECES,),
            in_specs=[pl.BlockSpec((rows, units), lambda j, place: (0, 0))] * CHIPS
            + [
                pl.BlockSpec((ranks, depth, piece), lambda j, place: (0, 0, j)),
                pl.BlockSpec(order.shape, lambda j, place: (0, 0)),
            ],
            out_specs=pl.BlockSpec((rows * PIECES, piece), lambda j, place: (0, 0)),
            scratch_shapes=[pltpu.VMEM((PIECES, rows, piece), bf16)],
        ),
        out_shape=jax.ShapeDtypeStruct((rows * PIECES, piece), bf16),
        compiler_params=roomy,
        name="down_rows",
    )(place, *hidden, w_down, order)


def finish_kernel(back0, back1, weights0, weights1, stream, logits, out):
    moe = stream[...].astype(f32)
    for back, weights in ((back0, weights0), (back1, weights1)):
        high = weights[...].astype(bf16)
        low = (weights[...] - high.astype(f32)).astype(bf16)
        moe = moe + (
            jnp.dot(high, back[...], preferred_element_type=f32)
            + jnp.dot(low, back[...], preferred_element_type=f32)
        )
    rows = stream.shape[0]
    out[0:rows, :] = moe.astype(bf16)
    logit_high = logits[...].astype(bf16)
    logit_low = (logits[...] - logit_high.astype(f32)).astype(bf16)
    filler = jnp.zeros((logits.shape[0], out.shape[1] - 2 * logits.shape[1]), bf16)
    out[rows:, :] = jnp.concatenate([logit_high, logit_low, filler], axis=1)


def finish(returned, weights, stream, logits):
    return pl.pallas_call(
        finish_kernel,
        out_shape=jax.ShapeDtypeStruct(
            (stream.shape[0] + logits.shape[0], stream.shape[1]), bf16
        ),
        compiler_params=roomy,
        name="finish",
    )(*returned, *weights, stream, logits)


def assemble_kernel(place, same_core, other_core, mixed, logits):
    rows = mixed.shape[0] // (2 * CHIPS)
    piece = same_core.shape[2]
    count = logits.shape[1]
    for other, blocks in enumerate((same_core, other_core)):
        for shift in range(CHIPS):
            rank = 2 * ((place[0] + CHIPS - shift) % CHIPS) + (place[1] + other) % 2
            at = pl.ds(pl.multiple_of(rank * rows, rows), rows)
            for j in range(PIECES):
                mixed[at, j * piece : (j + 1) * piece] = blocks[
                    shift, j * rows : (j + 1) * rows, :
                ]
            tail = blocks[shift, PIECES * rows :, :].astype(f32)
            logits[at, :] = tail[:, :count] + tail[:, count : 2 * count]


def assemble(place, same_core, other_core, expert_count):
    rows = same_core.shape[1] // (PIECES + 1)
    width = same_core.shape[2] * PIECES
    whole = pl.BlockSpec(memory_space=pltpu.VMEM)
    return pl.pallas_call(
        assemble_kernel,
        in_specs=[pl.BlockSpec(memory_space=pltpu.SMEM), whole, whole],
        out_shape=(
            jax.ShapeDtypeStruct((rows * 2 * CHIPS, width), bf16),
            jax.ShapeDtypeStruct((rows * 2 * CHIPS, expert_count), f32),
        ),
        compiler_params=roomy,
        name="assemble",
    )(place, same_core, other_core)


def routing(chosen, combine, expert_count, capacity):
    targets = slot_targets(chosen, expert_count, capacity)
    tokens = chosen.shape[0]
    slots = capacity // HALVES
    run = PIECES * slots
    total = expert_count * run
    row = lax.broadcasted_iota(jnp.int32, (PIECES * tokens, total), 0)
    col = lax.broadcasted_iota(jnp.int32, (PIECES * tokens, total), 1)
    same_piece = row // tokens == (col % run) // slots
    targets = jnp.tile(targets, (PIECES, 1))
    combine = jnp.tile(combine, (PIECES, 1))
    results = []
    for half in range(HALVES):
        slot_of = col // run * capacity + half * slots + col % slots
        wanted = jnp.where(same_piece, slot_of, -1)
        weights = jnp.zeros((PIECES * tokens, total), f32)
        for k in range(chosen.shape[1]):
            weights = jnp.where(wanted == targets[:, k : k + 1], combine[:, k : k + 1], weights)
        results.append(weights)
    return results


def shards(
    attn_out,
    residual,
    o_weight,
    norm_gain,
    router_weight,
    expert_idx,
    combine,
    w_gate,
    w_up,
    w_down,
):
    ranks = lax.axis_size("tensor")
    rank = lax.axis_index("tensor")
    place = jnp.stack([rank // 2, rank % 2]).astype(jnp.int32)
    group_rows, width = residual.shape
    rows = group_rows // ranks
    expert_count = router_weight.shape[1]
    top_count = expert_idx.shape[1]
    capacity = min(rows, max(2, 3 * rows * top_count // (2 * expert_count)))
    slots = capacity // HALVES

    w_down_all = lax.all_gather(w_down[0], "tensor", axis=0, tiled=False)
    gate_own, up_own = w_gate[0].T, w_up[0].T
    weights = (gate_own, across(gate_own), up_own, across(up_own))
    order = reorder_matrix(PIECES, BATCH, slots)
    chosen = lax.dynamic_slice_in_dim(expert_idx, rank * rows, rows, 0)
    my_combine = lax.dynamic_slice_in_dim(combine, rank * rows, rows, 0)
    shares = routing(chosen, my_combine, expert_count, capacity)

    mine, theirs = project(place, attn_out, o_weight)
    sums = pair_sums(mine, across(theirs))
    parts = (sums[0],) + tuple(along(sums[shift], shift) for shift in range(1, CHIPS))
    outbox0, outbox1, stream, logits = front(
        place, parts, residual, norm_gain.reshape(1, width), router_weight.T, shares
    )
    arrived = []
    for outbox in (outbox0, outbox1):
        arrived.append(lax.all_to_all(outbox, "expert", split_axis=0, concat_axis=0, tiled=True))
    own = [rows_by_piece(x, order) for x in arrived]
    returned = []
    for half, (low, high) in enumerate(own):
        low_up, high_down = along(low, 1), along(high, -1)
        high_up, low_down = along(high, 1), along(low, -1)
        low_far, high_far = along(low_up, 1), along(high_down, -1)
        hidden = up_rows(
            (low, low_up, low_far, low_down),
            (high, high_up, high_far, high_down),
            weights,
            own[1][0] if half == 0 else own[0][0],
        )
        units = (hidden[0],) + tuple(along(hidden[s], -s) for s in range(1, CHIPS))
        expert_out = down_rows(place, units, w_down_all, order)
        returned.append(
            lax.all_to_all(expert_out, "expert", split_axis=0, concat_axis=0, tiled=True)
        )
    packed = finish(returned, shares, stream, logits)
    same_core = jnp.stack([packed] + [along(packed, shift) for shift in range(1, CHIPS)])
    return assemble(place, same_core, across(same_core), expert_count)


def solution(mesh):
    in_specs = (
        P("expert", "tensor"),
        P("expert", None),
        P("tensor", None),
        P(),
        P(),
        P("expert", None),
        P("expert", None),
        P("expert", None, "tensor"),
        P("expert", None, "tensor"),
        P("expert", "tensor", None),
    )
    out_specs = (P("expert", None), P("expert", None))

    return jax.shard_map(shards, mesh=mesh, in_specs=in_specs, out_specs=out_specs, check_vma=False)
```

```python
import jax
import jax.numpy as jnp
from jax import lax
from jax.experimental import pallas as pl
from jax.experimental.pallas import tpu as pltpu
from jax.sharding import PartitionSpec as P


epsilon = 1e-06
PIECES = 8
HALVES = 2
CHIPS = 4
BATCH = 16
f32 = jnp.float32
bf16 = jnp.bfloat16


def space(mebibytes):
    return pltpu.CompilerParams(vmem_limit_bytes=mebibytes * 2**20)


def slot_targets(chosen, expert_count, capacity):
    flat_ids = chosen.reshape(-1)
    one_hot = (flat_ids[:, None] == jnp.arange(expert_count, dtype=jnp.int32)[None, :]).astype(
        jnp.int32
    )
    slot_index = jnp.sum((jnp.cumsum(one_hot, axis=0) - 1) * one_hot, axis=1)
    return (flat_ids * capacity + slot_index).reshape(chosen.shape)


def reorder_matrix(outer, inner, run):
    size = outer * inner * run
    row = lax.broadcasted_iota(jnp.int32, (size, size), 0)
    col = lax.broadcasted_iota(jnp.int32, (size, size), 1)
    a = row // (inner * run)
    b = row % (inner * run) // run
    return (col == b * (outer * run) + a * run + row % run).astype(bf16)


def pieces_to_rows(x):
    width = x.shape[1] // PIECES
    return jnp.concatenate([x[:, j * width : (j + 1) * width] for j in range(PIECES)], axis=0)


def dot_last(a, b):
    return lax.dot_general(a, b, (((1,), (1,)), ((), ())), preferred_element_type=f32)


def dot_first(a, b):
    return lax.dot_general(a, b, (((0,), (0,)), ((), ())), preferred_element_type=f32)


def along(x, shift):
    pairs = [
        (2 * chip + core, 2 * ((chip + shift) % CHIPS) + core)
        for chip in range(CHIPS)
        for core in range(2)
    ]
    return lax.ppermute(x, "tensor", pairs)


def across(x):
    return lax.ppermute(x, "tensor", [(r, r ^ 1) for r in range(2 * CHIPS)])


def project_kernel(place, attn, weight, mine, theirs):
    rows = mine.shape[1]
    chip, core = place[0], place[1]

    def block(shift, other):
        rank = 2 * ((chip + shift) % CHIPS) + (core + other) % 2
        return attn[pl.ds(pl.multiple_of(rank * rows, rows), rows), :]

    ordered = [block(shift, other) for other in range(2) for shift in range(CHIPS)]
    total = jnp.dot(
        jnp.concatenate(ordered, axis=0), weight[...], preferred_element_type=f32
    ).astype(bf16)
    for i in range(CHIPS):
        mine[i] = total[i * rows : (i + 1) * rows, :]
        theirs[i] = total[(CHIPS + i) * rows : (CHIPS + i + 1) * rows, :]


def project(place, attn, weight):
    depth, width = weight.shape
    rows = attn.shape[0] // (2 * CHIPS)
    step = width // 4
    out = jax.ShapeDtypeStruct((CHIPS, rows, width), bf16)
    return pl.pallas_call(
        project_kernel,
        grid_spec=pltpu.PrefetchScalarGridSpec(
            num_scalar_prefetch=1,
            grid=(4,),
            in_specs=[
                pl.BlockSpec(attn.shape, lambda n, place: (0, 0)),
                pl.BlockSpec((depth, step), lambda n, place: (0, n)),
            ],
            out_specs=[pl.BlockSpec((CHIPS, rows, step), lambda n, place: (0, 0, n))] * 2,
        ),
        out_shape=(out, out),
        compiler_params=space(8),
        name="project",
    )(place, attn, weight)


def pair_kernel(mine, other, *outs):
    for i in range(CHIPS):
        outs[i][...] = (mine[i].astype(f32) + other[i].astype(f32)).astype(bf16)


def pair_sums(mine, other):
    out = jax.ShapeDtypeStruct(mine.shape[1:], bf16)
    return pl.pallas_call(
        pair_kernel, out_shape=(out,) * CHIPS, compiler_params=space(6), name="pair_sums"
    )(mine, other)


def front_kernel(place, p0, p1, p2, p3, residual, gain, router, shares0, shares1, _, *outs):
    outbox0, outbox1, stream_out, logits_out = outs
    rows = p0.shape[0]
    start = (2 * place[0] + place[1]) * rows
    total = (p0[...].astype(f32) + p1[...].astype(f32)) + (
        p2[...].astype(f32) + p3[...].astype(f32)
    )
    mine = residual[pl.ds(pl.multiple_of(start, rows), rows), :]
    stream = (mine.astype(f32) + total).astype(bf16)
    wide = stream.astype(f32)
    scale = lax.rsqrt(jnp.mean(wide * wide, axis=-1, keepdims=True) + epsilon)
    normed = (wide * scale * gain[...]).astype(bf16)
    stream_out[...] = pieces_to_rows(stream)
    logits_out[...] = dot_last(normed, router[...])
    by_piece = pieces_to_rows(normed)
    for shares, outbox in ((shares0, outbox0), (shares1, outbox1)):
        hits = (shares[...] != 0.0).astype(bf16)
        outbox[...] = dot_first(hits, by_piece).astype(bf16)


def front(place, parts, residual, gain, router, shares, after):
    rows, width = parts[0].shape
    piece = width // PIECES
    whole = pl.BlockSpec(memory_space=pltpu.VMEM)
    outbox = jax.ShapeDtypeStruct((shares[0].shape[1], piece), bf16)
    return pl.pallas_call(
        front_kernel,
        in_specs=[pl.BlockSpec(memory_space=pltpu.SMEM)]
        + [whole] * 9
        + [pl.BlockSpec(memory_space=pl.ANY)],
        out_shape=(
            outbox,
            outbox,
            jax.ShapeDtypeStruct((rows * PIECES, piece), bf16),
            jax.ShapeDtypeStruct((rows, router.shape[0]), f32),
        ),
        compiler_params=space(10),
        name="front",
    )(place, *parts, residual, gain, router, *shares, after)


def by_piece_kernel(x, order, out):
    moved = jnp.dot(order[...], x[...], preferred_element_type=f32)
    out[...] = moved.reshape(out.shape).astype(bf16)


def rows_by_piece(x, order):
    size = order.shape[0]
    steps = x.shape[0] // size
    width = x.shape[1]
    run = size // PIECES
    return pl.pallas_call(
        by_piece_kernel,
        grid=(steps,),
        in_specs=[
            pl.BlockSpec((size, width), lambda a: (a, 0)),
            pl.BlockSpec((size, size), lambda a: (0, 0)),
        ],
        out_specs=pl.BlockSpec((PIECES, run, width), lambda a: (0, a, 0)),
        out_shape=jax.ShapeDtypeStruct((PIECES, run * steps, width), bf16),
        compiler_params=space(6),
        name="rows_by_piece",
    )(x, order)


def up_kernel(own, back, ahead, far_low, far_high, *refs):
    gate_own, gate_other, up_own, up_other, _, *outs, gate, up = refs
    step = pl.program_id(0)
    width = own.shape[2]

    @pl.when(step == 0)
    def _():
        gate[...] = jnp.zeros_like(gate)
        up[...] = jnp.zeros_like(up)

    for q in range(own.shape[0]):
        far = jnp.where(step == 0, far_low[q], far_high[q])
        x = jnp.concatenate([own[q], back[q], far, ahead[q]], axis=0)
        at = slice(q * width, (q + 1) * width)
        gate[...] += dot_last(x, jnp.concatenate([gate_own[:, at], gate_other[:, at]], axis=0))
        up[...] += dot_last(x, jnp.concatenate([up_own[:, at], up_other[:, at]], axis=0))

    @pl.when(step == pl.num_programs(0) - 1)
    def _():
        g = gate[...]
        hidden = (g / (1.0 + jnp.exp(-g)) * up[...]).astype(bf16)
        rows = outs[0].shape[0]
        for i in range(CHIPS):
            outs[i][...] = hidden[i * rows : (i + 1) * rows, :]


def up_rows(own, back, ahead, far, weights, after):
    pieces, rows, width = own.shape
    half = pieces // 2
    units = weights[0].shape[0]
    out = jax.ShapeDtypeStruct((rows, 2 * units), bf16)
    return pl.pallas_call(
        up_kernel,
        grid=(2,),
        in_specs=[pl.BlockSpec((half, rows, width), lambda j: (j, 0, 0))] * 3
        + [pl.BlockSpec((half, rows, width), lambda j: (0, 0, 0))] * 2
        + [pl.BlockSpec((units, half * width), lambda j: (0, j))] * 4
        + [pl.BlockSpec(memory_space=pl.ANY)],
        out_specs=[pl.BlockSpec((rows, 2 * units), lambda j: (0, 0))] * CHIPS,
        out_shape=(out,) * CHIPS,
        scratch_shapes=[pltpu.VMEM((CHIPS * rows, 2 * units), f32)] * 2,
        compiler_params=space(15),
        name="up_rows",
    )(own, back, ahead, *far, *weights, after)


def down_kernel(*refs):
    hidden, refs = refs[:CHIPS], refs[CHIPS:]
    weights, (order, out, held) = refs[: 2 * CHIPS], refs[2 * CHIPS :]
    step = pl.program_id(0)
    total = None
    for i in range(CHIPS):
        weight = jnp.concatenate([weights[2 * i][...], weights[2 * i + 1][...]], axis=0)
        part = jnp.dot(hidden[i][...], weight, preferred_element_type=f32)
        total = part if total is None else total + part
    total = total.astype(bf16)
    width = held.shape[2]
    count = total.shape[1] // width
    for q in range(count):
        held[step * count + q] = total[:, q * width : (q + 1) * width]

    @pl.when(step == pl.num_programs(0) - 1)
    def _():
        size = order.shape[0]
        run = size // PIECES
        for a in range(held.shape[1] // run):
            block = held[:, a * run : (a + 1) * run, :].reshape(size, width)
            out[a * size : (a + 1) * size, :] = dot_first(order[...], block).astype(bf16)


def down_rows(hidden, weights, order):
    rows, units = hidden[0].shape
    depth, width = weights[0].shape
    piece = width // PIECES
    steps = 4
    return pl.pallas_call(
        down_kernel,
        grid=(steps,),
        in_specs=[pl.BlockSpec((rows, units), lambda j: (0, 0))] * CHIPS
        + [pl.BlockSpec((depth, width // steps), lambda j: (0, j))] * (2 * CHIPS)
        + [pl.BlockSpec(order.shape, lambda j: (0, 0))],
        out_specs=pl.BlockSpec((rows * PIECES, piece), lambda j: (0, 0)),
        out_shape=jax.ShapeDtypeStruct((rows * PIECES, piece), bf16),
        scratch_shapes=[pltpu.VMEM((PIECES, rows, piece), bf16)],
        compiler_params=space(11),
        name="down_rows",
    )(*hidden, *weights, order)


def finish_kernel(back0, back1, weights0, weights1, stream, logits, out):
    moe = stream[...].astype(f32)
    for back, weights in ((back0, weights0), (back1, weights1)):
        high = weights[...].astype(bf16)
        low = (weights[...] - high.astype(f32)).astype(bf16)
        moe = moe + (
            jnp.dot(high, back[...], preferred_element_type=f32)
            + jnp.dot(low, back[...], preferred_element_type=f32)
        )
    rows = stream.shape[0]
    out[0:rows, :] = moe.astype(bf16)
    logit_high = logits[...].astype(bf16)
    logit_low = (logits[...] - logit_high.astype(f32)).astype(bf16)
    filler = jnp.zeros((logits.shape[0], out.shape[1] - 2 * logits.shape[1]), bf16)
    out[rows:, :] = jnp.concatenate([logit_high, logit_low, filler], axis=1)


def finish(returned, weights, stream, logits):
    return pl.pallas_call(
        finish_kernel,
        out_shape=jax.ShapeDtypeStruct(
            (stream.shape[0] + logits.shape[0], stream.shape[1]), bf16
        ),
        compiler_params=space(6),
        name="finish",
    )(*returned, *weights, stream, logits)


def assemble_kernel(place, same_core, other_core, mixed, logits):
    rows = mixed.shape[0] // (2 * CHIPS)
    piece = same_core.shape[2]
    count = logits.shape[1]
    for other, blocks in enumerate((same_core, other_core)):
        for shift in range(CHIPS):
            rank = 2 * ((place[0] + CHIPS - shift) % CHIPS) + (place[1] + other) % 2
            at = pl.ds(pl.multiple_of(rank * rows, rows), rows)
            for j in range(PIECES):
                mixed[at, j * piece : (j + 1) * piece] = blocks[
                    shift, j * rows : (j + 1) * rows, :
                ]
            tail = blocks[shift, PIECES * rows :, :].astype(f32)
            logits[at, :] = tail[:, :count] + tail[:, count : 2 * count]


def assemble(place, same_core, other_core, expert_count):
    rows = same_core.shape[1] // (PIECES + 1)
    width = same_core.shape[2] * PIECES
    whole = pl.BlockSpec(memory_space=pltpu.VMEM)
    return pl.pallas_call(
        assemble_kernel,
        in_specs=[pl.BlockSpec(memory_space=pltpu.SMEM), whole, whole],
        out_shape=(
            jax.ShapeDtypeStruct((rows * 2 * CHIPS, width), bf16),
            jax.ShapeDtypeStruct((rows * 2 * CHIPS, expert_count), f32),
        ),
        compiler_params=space(6),
        name="assemble",
    )(place, same_core, other_core)


def routing(chosen, combine, expert_count, capacity):
    targets = slot_targets(chosen, expert_count, capacity)
    tokens = chosen.shape[0]
    slots = capacity // HALVES
    run = PIECES * slots
    total = expert_count * run
    row = lax.broadcasted_iota(jnp.int32, (PIECES * tokens, total), 0)
    col = lax.broadcasted_iota(jnp.int32, (PIECES * tokens, total), 1)
    same_piece = row // tokens == (col % run) // slots
    targets = jnp.tile(targets, (PIECES, 1))
    combine = jnp.tile(combine, (PIECES, 1))
    results = []
    for half in range(HALVES):
        slot_of = col // run * capacity + half * slots + col % slots
        wanted = jnp.where(same_piece, slot_of, -1)
        weights = jnp.zeros((PIECES * tokens, total), f32)
        for k in range(chosen.shape[1]):
            weights = jnp.where(wanted == targets[:, k : k + 1], combine[:, k : k + 1], weights)
        results.append(weights)
    return results


def shards(
    attn_out,
    residual,
    o_weight,
    norm_gain,
    router_weight,
    expert_idx,
    combine,
    w_gate,
    w_up,
    w_down,
):
    ranks = lax.axis_size("tensor")
    rank = lax.axis_index("tensor")
    place = jnp.stack([rank // 2, rank % 2]).astype(jnp.int32)
    group_rows, width = residual.shape
    rows = group_rows // ranks
    expert_count = router_weight.shape[1]
    top_count = expert_idx.shape[1]
    capacity = min(rows, max(2, 3 * rows * top_count // (2 * expert_count)))
    slots = capacity // HALVES

    same_core = [w_down[0]] + [along(w_down[0], shift) for shift in range(1, CHIPS)]
    gate_own, up_own = w_gate[0].T, w_up[0].T
    weights = (gate_own, across(gate_own), up_own, across(up_own))
    order = reorder_matrix(PIECES, BATCH, slots)
    chosen = lax.dynamic_slice_in_dim(expert_idx, rank * rows, rows, 0)
    my_combine = lax.dynamic_slice_in_dim(combine, rank * rows, rows, 0)
    shares = routing(chosen, my_combine, expert_count, capacity)

    mine, theirs = project(place, attn_out, o_weight)
    sums = pair_sums(mine, across(theirs))
    parts = (sums[0],) + tuple(along(sums[shift], shift) for shift in range(1, CHIPS))
    down_weights = []
    for shift in range(CHIPS):
        weight = same_core[-shift % CHIPS]
        down_weights += [weight, across(weight)]
    outbox0, outbox1, stream, logits = front(
        place, parts, residual, norm_gain.reshape(1, width), router_weight.T, shares, order
    )
    arrived = []
    for outbox in (outbox0, outbox1):
        arrived.append(lax.all_to_all(outbox, "expert", split_axis=0, concat_axis=0, tiled=True))
    own = []
    for x in arrived:
        own.append(rows_by_piece(x, order))
    returned = []
    for half, mine in enumerate(own):
        back, ahead = along(mine, 1), along(mine, -1)
        far = (along(back[: PIECES // 2], 1), along(ahead[PIECES // 2 :], -1))
        hidden = up_rows(mine, back, ahead, far, weights, own[1 - half])
        units = (hidden[0],) + tuple(along(hidden[s], -s) for s in range(1, CHIPS))
        expert_out = down_rows(units, down_weights, order)
        returned.append(
            lax.all_to_all(expert_out, "expert", split_axis=0, concat_axis=0, tiled=True)
        )
    packed = finish(returned, shares, stream, logits)
    same_core = jnp.stack([packed] + [along(packed, shift) for shift in range(1, CHIPS)])
    return assemble(place, same_core, across(same_core), expert_count)


def solution(mesh):
    in_specs = (
        P("expert", "tensor"),
        P("expert", None),
        P("tensor", None),
        P(),
        P(),
        P("expert", None),
        P("expert", None),
        P("expert", None, "tensor"),
        P("expert", None, "tensor"),
        P("expert", "tensor", None),
    )
    out_specs = (P("expert", None), P("expert", None))

    return jax.shard_map(shards, mesh=mesh, in_specs=in_specs, out_specs=out_specs, check_vma=False)
```

```python
import jax
import jax.numpy as jnp
from jax import lax
from jax.experimental import pallas as pl
from jax.experimental.pallas import tpu as pltpu
from jax.sharding import PartitionSpec as P


epsilon = 1e-06
PIECES = 8
HALVES = 2
CHIPS = 4
BATCH = 16
f32 = jnp.float32
bf16 = jnp.bfloat16


def space(mebibytes):
    return pltpu.CompilerParams(vmem_limit_bytes=mebibytes * 2**20)


def slot_targets(chosen, expert_count, capacity):
    flat_ids = chosen.reshape(-1)
    one_hot = (flat_ids[:, None] == jnp.arange(expert_count, dtype=jnp.int32)[None, :]).astype(
        jnp.int32
    )
    slot_index = jnp.sum((jnp.cumsum(one_hot, axis=0) - 1) * one_hot, axis=1)
    return (flat_ids * capacity + slot_index).reshape(chosen.shape)


def reorder_matrix(outer, inner, run):
    size = outer * inner * run
    row = lax.broadcasted_iota(jnp.int32, (size, size), 0)
    col = lax.broadcasted_iota(jnp.int32, (size, size), 1)
    a = row // (inner * run)
    b = row % (inner * run) // run
    return (col == b * (outer * run) + a * run + row % run).astype(bf16)


def pieces_to_rows(x):
    width = x.shape[1] // PIECES
    return jnp.concatenate([x[:, j * width : (j + 1) * width] for j in range(PIECES)], axis=0)


def dot_last(a, b):
    return lax.dot_general(a, b, (((1,), (1,)), ((), ())), preferred_element_type=f32)


def dot_first(a, b):
    return lax.dot_general(a, b, (((0,), (0,)), ((), ())), preferred_element_type=f32)


def along(x, shift):
    pairs = [
        (2 * chip + core, 2 * ((chip + shift) % CHIPS) + core)
        for chip in range(CHIPS)
        for core in range(2)
    ]
    return lax.ppermute(x, "tensor", pairs)


def around(x, sign):
    pairs = [
        (2 * chip + core, 2 * ((chip + (sign if core == 0 else -sign)) % CHIPS) + core)
        for chip in range(CHIPS)
        for core in range(2)
    ]
    return lax.ppermute(x, "tensor", pairs)


def across(x):
    return lax.ppermute(x, "tensor", [(r, r ^ 1) for r in range(2 * CHIPS)])


def project_kernel(place, attn, weight, mine, theirs):
    rows = mine.shape[1]
    chip, core = place[0], place[1]

    def block(shift, other):
        rank = 2 * ((chip + shift) % CHIPS) + (core + other) % 2
        return attn[pl.ds(pl.multiple_of(rank * rows, rows), rows), :]

    ordered = [block(shift, other) for other in range(2) for shift in range(CHIPS)]
    total = jnp.dot(
        jnp.concatenate(ordered, axis=0), weight[...], preferred_element_type=f32
    ).astype(bf16)
    for i in range(CHIPS):
        mine[i] = total[i * rows : (i + 1) * rows, :]
        theirs[i] = total[(CHIPS + i) * rows : (CHIPS + i + 1) * rows, :]


def project(place, attn, weight):
    depth, width = weight.shape
    rows = attn.shape[0] // (2 * CHIPS)
    step = width // 4
    out = jax.ShapeDtypeStruct((CHIPS, rows, width), bf16)
    return pl.pallas_call(
        project_kernel,
        grid_spec=pltpu.PrefetchScalarGridSpec(
            num_scalar_prefetch=1,
            grid=(4,),
            in_specs=[
                pl.BlockSpec(attn.shape, lambda n, place: (0, 0)),
                pl.BlockSpec((depth, step), lambda n, place: (0, n)),
            ],
            out_specs=[pl.BlockSpec((CHIPS, rows, step), lambda n, place: (0, 0, n))] * 2,
        ),
        out_shape=(out, out),
        compiler_params=space(8),
        name="project",
    )(place, attn, weight)


def pair_kernel(mine, other, *outs):
    for i in range(CHIPS):
        outs[i][...] = (mine[i].astype(f32) + other[i].astype(f32)).astype(bf16)


def pair_sums(mine, other):
    out = jax.ShapeDtypeStruct(mine.shape[1:], bf16)
    return pl.pallas_call(
        pair_kernel, out_shape=(out,) * CHIPS, compiler_params=space(6), name="pair_sums"
    )(mine, other)


def front_kernel(place, p0, p1, p2, p3, residual, gain, router, shares0, shares1, _, *outs):
    outbox0, outbox1, stream_out, logits_out = outs
    rows = p0.shape[0]
    start = (2 * place[0] + place[1]) * rows
    total = (p0[...].astype(f32) + p1[...].astype(f32)) + (
        p2[...].astype(f32) + p3[...].astype(f32)
    )
    mine = residual[pl.ds(pl.multiple_of(start, rows), rows), :]
    stream = (mine.astype(f32) + total).astype(bf16)
    wide = stream.astype(f32)
    scale = lax.rsqrt(jnp.mean(wide * wide, axis=-1, keepdims=True) + epsilon)
    normed = (wide * scale * gain[...]).astype(bf16)
    stream_out[...] = pieces_to_rows(stream)
    logits_out[...] = dot_last(normed, router[...])
    by_piece = pieces_to_rows(normed)
    for shares, outbox in ((shares0, outbox0), (shares1, outbox1)):
        hits = (shares[...] != 0.0).astype(bf16)
        outbox[...] = dot_first(hits, by_piece).astype(bf16)


def front(place, parts, residual, gain, router, shares, after):
    rows, width = parts[0].shape
    piece = width // PIECES
    whole = pl.BlockSpec(memory_space=pltpu.VMEM)
    outbox = jax.ShapeDtypeStruct((shares[0].shape[1], piece), bf16)
    return pl.pallas_call(
        front_kernel,
        in_specs=[pl.BlockSpec(memory_space=pltpu.SMEM)]
        + [whole] * 9
        + [pl.BlockSpec(memory_space=pl.ANY)],
        out_shape=(
            outbox,
            outbox,
            jax.ShapeDtypeStruct((rows * PIECES, piece), bf16),
            jax.ShapeDtypeStruct((rows, router.shape[0]), f32),
        ),
        compiler_params=space(10),
        name="front",
    )(place, *parts, residual, gain, router, *shares, after)


def by_piece_kernel(x, order, out):
    moved = jnp.dot(order[...], x[...], preferred_element_type=f32)
    out[...] = moved.reshape(out.shape).astype(bf16)


def rows_by_piece(x, order):
    size = order.shape[0]
    steps = x.shape[0] // size
    width = x.shape[1]
    run = size // PIECES
    return pl.pallas_call(
        by_piece_kernel,
        grid=(steps,),
        in_specs=[
            pl.BlockSpec((size, width), lambda a: (a, 0)),
            pl.BlockSpec((size, size), lambda a: (0, 0)),
        ],
        out_specs=pl.BlockSpec((PIECES, run, width), lambda a: (0, a, 0)),
        out_shape=jax.ShapeDtypeStruct((PIECES, run * steps, width), bf16),
        compiler_params=space(6),
        name="rows_by_piece",
    )(x, order)


def up_kernel(r0, r1, r2, r3, gate_own, gate_other, up_own, up_other, *refs):
    *outs, gate, up = refs
    step = pl.program_id(0)
    width = r0.shape[2]

    @pl.when(step == 0)
    def _():
        gate[...] = jnp.zeros_like(gate)
        up[...] = jnp.zeros_like(up)

    for q in range(r0.shape[0]):
        x = jnp.concatenate([r0[q], r1[q], r2[q], r3[q]], axis=0)
        at = slice(q * width, (q + 1) * width)
        gate[...] += dot_last(x, jnp.concatenate([gate_own[:, at], gate_other[:, at]], axis=0))
        up[...] += dot_last(x, jnp.concatenate([up_own[:, at], up_other[:, at]], axis=0))

    @pl.when(step == pl.num_programs(0) - 1)
    def _():
        g = gate[...]
        hidden = (g / (1.0 + jnp.exp(-g)) * up[...]).astype(bf16)
        rows = outs[0].shape[0]
        for i in range(CHIPS):
            outs[i][...] = hidden[i * rows : (i + 1) * rows, :]


def up_rows(sources, weights):
    pieces, rows, width = sources[0].shape
    half = pieces // 2
    units = weights[0].shape[0]
    out = jax.ShapeDtypeStruct((rows, 2 * units), bf16)
    return pl.pallas_call(
        up_kernel,
        grid=(2,),
        in_specs=[pl.BlockSpec((half, rows, width), lambda j: (j, 0, 0))] * CHIPS
        + [pl.BlockSpec((units, half * width), lambda j: (0, j))] * 4,
        out_specs=[pl.BlockSpec((rows, 2 * units), lambda j: (0, 0))] * CHIPS,
        out_shape=(out,) * CHIPS,
        scratch_shapes=[pltpu.VMEM((CHIPS * rows, 2 * units), f32)] * 2,
        compiler_params=space(15),
        name="up_rows",
    )(*sources, *weights)


def down_kernel(*refs):
    hidden, refs = refs[:CHIPS], refs[CHIPS:]
    weights, (order, out, held) = refs[: 2 * CHIPS], refs[2 * CHIPS :]
    step = pl.program_id(0)
    total = None
    for i in range(CHIPS):
        weight = jnp.concatenate([weights[2 * i][...], weights[2 * i + 1][...]], axis=0)
        part = jnp.dot(hidden[i][...], weight, preferred_element_type=f32)
        total = part if total is None else total + part
    total = total.astype(bf16)
    width = held.shape[2]
    count = total.shape[1] // width
    for q in range(count):
        held[step * count + q] = total[:, q * width : (q + 1) * width]

    @pl.when(step == pl.num_programs(0) - 1)
    def _():
        size = order.shape[0]
        run = size // PIECES
        for a in range(held.shape[1] // run):
            block = held[:, a * run : (a + 1) * run, :].reshape(size, width)
            out[a * size : (a + 1) * size, :] = dot_first(order[...], block).astype(bf16)


def down_rows(hidden, weights, order):
    rows, units = hidden[0].shape
    depth, width = weights[0].shape
    piece = width // PIECES
    steps = 4
    return pl.pallas_call(
        down_kernel,
        grid=(steps,),
        in_specs=[pl.BlockSpec((rows, units), lambda j: (0, 0))] * CHIPS
        + [pl.BlockSpec((depth, width // steps), lambda j: (0, j))] * (2 * CHIPS)
        + [pl.BlockSpec(order.shape, lambda j: (0, 0))],
        out_specs=pl.BlockSpec((rows * PIECES, piece), lambda j: (0, 0)),
        out_shape=jax.ShapeDtypeStruct((rows * PIECES, piece), bf16),
        scratch_shapes=[pltpu.VMEM((PIECES, rows, piece), bf16)],
        compiler_params=space(11),
        name="down_rows",
    )(*hidden, *weights, order)


def finish_kernel(back0, back1, weights0, weights1, stream, logits, out):
    moe = stream[...].astype(f32)
    for back, weights in ((back0, weights0), (back1, weights1)):
        high = weights[...].astype(bf16)
        low = (weights[...] - high.astype(f32)).astype(bf16)
        moe = moe + (
            jnp.dot(high, back[...], preferred_element_type=f32)
            + jnp.dot(low, back[...], preferred_element_type=f32)
        )
    rows = stream.shape[0]
    out[0:rows, :] = moe.astype(bf16)
    logit_high = logits[...].astype(bf16)
    logit_low = (logits[...] - logit_high.astype(f32)).astype(bf16)
    filler = jnp.zeros((logits.shape[0], out.shape[1] - 2 * logits.shape[1]), bf16)
    out[rows:, :] = jnp.concatenate([logit_high, logit_low, filler], axis=1)


def finish(returned, weights, stream, logits):
    return pl.pallas_call(
        finish_kernel,
        out_shape=jax.ShapeDtypeStruct(
            (stream.shape[0] + logits.shape[0], stream.shape[1]), bf16
        ),
        compiler_params=space(6),
        name="finish",
    )(*returned, *weights, stream, logits)


def assemble_kernel(place, same_core, other_core, mixed, logits):
    rows = mixed.shape[0] // (2 * CHIPS)
    piece = same_core.shape[2]
    count = logits.shape[1]
    for other, blocks in enumerate((same_core, other_core)):
        for shift in range(CHIPS):
            rank = 2 * ((place[0] + CHIPS - shift) % CHIPS) + (place[1] + other) % 2
            at = pl.ds(pl.multiple_of(rank * rows, rows), rows)
            for j in range(PIECES):
                mixed[at, j * piece : (j + 1) * piece] = blocks[
                    shift, j * rows : (j + 1) * rows, :
                ]
            tail = blocks[shift, PIECES * rows :, :].astype(f32)
            logits[at, :] = tail[:, :count] + tail[:, count : 2 * count]


def assemble(place, same_core, other_core, expert_count):
    rows = same_core.shape[1] // (PIECES + 1)
    width = same_core.shape[2] * PIECES
    whole = pl.BlockSpec(memory_space=pltpu.VMEM)
    return pl.pallas_call(
        assemble_kernel,
        in_specs=[pl.BlockSpec(memory_space=pltpu.SMEM), whole, whole],
        out_shape=(
            jax.ShapeDtypeStruct((rows * 2 * CHIPS, width), bf16),
            jax.ShapeDtypeStruct((rows * 2 * CHIPS, expert_count), f32),
        ),
        compiler_params=space(6),
        name="assemble",
    )(place, same_core, other_core)


def routing(chosen, combine, expert_count, capacity):
    targets = slot_targets(chosen, expert_count, capacity)
    tokens = chosen.shape[0]
    slots = capacity // HALVES
    run = PIECES * slots
    total = expert_count * run
    row = lax.broadcasted_iota(jnp.int32, (PIECES * tokens, total), 0)
    col = lax.broadcasted_iota(jnp.int32, (PIECES * tokens, total), 1)
    same_piece = row // tokens == (col % run) // slots
    targets = jnp.tile(targets, (PIECES, 1))
    combine = jnp.tile(combine, (PIECES, 1))
    results = []
    for half in range(HALVES):
        slot_of = col // run * capacity + half * slots + col % slots
        wanted = jnp.where(same_piece, slot_of, -1)
        weights = jnp.zeros((PIECES * tokens, total), f32)
        for k in range(chosen.shape[1]):
            weights = jnp.where(wanted == targets[:, k : k + 1], combine[:, k : k + 1], weights)
        results.append(weights)
    return results


def shards(
    attn_out,
    residual,
    o_weight,
    norm_gain,
    router_weight,
    expert_idx,
    combine,
    w_gate,
    w_up,
    w_down,
):
    ranks = lax.axis_size("tensor")
    rank = lax.axis_index("tensor")
    place = jnp.stack([rank // 2, rank % 2]).astype(jnp.int32)
    group_rows, width = residual.shape
    rows = group_rows // ranks
    expert_count = router_weight.shape[1]
    top_count = expert_idx.shape[1]
    capacity = min(rows, max(2, 3 * rows * top_count // (2 * expert_count)))
    slots = capacity // HALVES

    down_next = around(w_down[0], 1)
    down_far, down_last = around(down_next, 1), around(w_down[0], -1)
    gate_own, up_own = w_gate[0].T, w_up[0].T
    weights = (gate_own, across(gate_own), up_own, across(up_own))
    order = reorder_matrix(PIECES, BATCH, slots)
    chosen = lax.dynamic_slice_in_dim(expert_idx, rank * rows, rows, 0)
    my_combine = lax.dynamic_slice_in_dim(combine, rank * rows, rows, 0)
    shares = routing(chosen, my_combine, expert_count, capacity)

    mine, theirs = project(place, attn_out, o_weight)
    sums = pair_sums(mine, across(theirs))
    parts = (sums[0],) + tuple(along(sums[shift], shift) for shift in range(1, CHIPS))
    down_weights = [
        w_down[0],
        across(w_down[0]),
        down_next,
        across(down_last),
        down_far,
        across(down_far),
        down_last,
        across(down_next),
    ]
    outbox0, outbox1, stream, logits = front(
        place, parts, residual, norm_gain.reshape(1, width), router_weight.T, shares, order
    )
    arrived = []
    for outbox in (outbox0, outbox1):
        arrived.append(lax.all_to_all(outbox, "expert", split_axis=0, concat_axis=0, tiled=True))
    own = []
    for x in arrived:
        own.append(rows_by_piece(x, order))
    returned = []
    for mine in own:
        following = around(mine, 1)
        last = around(mine, -1)
        far = around(following, 1)
        hidden = up_rows((mine, following, far, last), weights)
        units = (
            hidden[0],
            around(hidden[3], 1),
            along(hidden[2], 2),
            around(hidden[1], -1),
        )
        expert_out = down_rows(units, down_weights, order)
        returned.append(
            lax.all_to_all(expert_out, "expert", split_axis=0, concat_axis=0, tiled=True)
        )
    packed = finish(returned, shares, stream, logits)
    same_core = jnp.stack([packed] + [along(packed, shift) for shift in range(1, CHIPS)])
    return assemble(place, same_core, across(same_core), expert_count)


def solution(mesh):
    in_specs = (
        P("expert", "tensor"),
        P("expert", None),
        P("tensor", None),
        P(),
        P(),
        P("expert", None),
        P("expert", None),
        P("expert", None, "tensor"),
        P("expert", None, "tensor"),
        P("expert", "tensor", None),
    )
    out_specs = (P("expert", None), P("expert", None))

    return jax.shard_map(shards, mesh=mesh, in_specs=in_specs, out_specs=out_specs, check_vma=False)
```

```python
import jax
import jax.numpy as jnp
from jax import lax
from jax.experimental import pallas as pl
from jax.experimental.pallas import tpu as pltpu
from jax.sharding import PartitionSpec as P


epsilon = 1e-06
PIECES = 8
HALVES = 2
CHIPS = 4
BATCH = 16
f32 = jnp.float32
bf16 = jnp.bfloat16


def space(mebibytes):
    return pltpu.CompilerParams(vmem_limit_bytes=mebibytes * 2**20)


def slot_targets(chosen, expert_count, capacity):
    flat_ids = chosen.reshape(-1)
    one_hot = (flat_ids[:, None] == jnp.arange(expert_count, dtype=jnp.int32)[None, :]).astype(
        jnp.int32
    )
    slot_index = jnp.sum((jnp.cumsum(one_hot, axis=0) - 1) * one_hot, axis=1)
    return (flat_ids * capacity + slot_index).reshape(chosen.shape)


def reorder_matrix(outer, inner, run):
    size = outer * inner * run
    row = lax.broadcasted_iota(jnp.int32, (size, size), 0)
    col = lax.broadcasted_iota(jnp.int32, (size, size), 1)
    a = row // (inner * run)
    b = row % (inner * run) // run
    return (col == b * (outer * run) + a * run + row % run).astype(bf16)


def pieces_to_rows(x):
    width = x.shape[1] // PIECES
    return jnp.concatenate([x[:, j * width : (j + 1) * width] for j in range(PIECES)], axis=0)


def dot_last(a, b):
    return lax.dot_general(a, b, (((1,), (1,)), ((), ())), preferred_element_type=f32)


def dot_first(a, b):
    return lax.dot_general(a, b, (((0,), (0,)), ((), ())), preferred_element_type=f32)


def along(x, shift):
    pairs = [
        (2 * chip + core, 2 * ((chip + shift) % CHIPS) + core)
        for chip in range(CHIPS)
        for core in range(2)
    ]
    return lax.ppermute(x, "tensor", pairs)


def around(x, sign):
    pairs = [
        (2 * chip + core, 2 * ((chip + (sign if core == 0 else -sign)) % CHIPS) + core)
        for chip in range(CHIPS)
        for core in range(2)
    ]
    return lax.ppermute(x, "tensor", pairs)


def across(x):
    return lax.ppermute(x, "tensor", [(r, r ^ 1) for r in range(2 * CHIPS)])


def project_kernel(place, attn, weight, mine, theirs):
    rows = mine.shape[1]
    chip, core = place[0], place[1]

    def block(shift, other):
        rank = 2 * ((chip + shift) % CHIPS) + (core + other) % 2
        return attn[pl.ds(pl.multiple_of(rank * rows, rows), rows), :]

    ordered = [block(shift, other) for other in range(2) for shift in range(CHIPS)]
    total = jnp.dot(
        jnp.concatenate(ordered, axis=0), weight[...], preferred_element_type=f32
    ).astype(bf16)
    for i in range(CHIPS):
        mine[i] = total[i * rows : (i + 1) * rows, :]
        theirs[i] = total[(CHIPS + i) * rows : (CHIPS + i + 1) * rows, :]


def project(place, attn, weight):
    depth, width = weight.shape
    rows = attn.shape[0] // (2 * CHIPS)
    step = width // 4
    out = jax.ShapeDtypeStruct((CHIPS, rows, width), bf16)
    return pl.pallas_call(
        project_kernel,
        grid_spec=pltpu.PrefetchScalarGridSpec(
            num_scalar_prefetch=1,
            grid=(4,),
            in_specs=[
                pl.BlockSpec(attn.shape, lambda n, place: (0, 0)),
                pl.BlockSpec((depth, step), lambda n, place: (0, n)),
            ],
            out_specs=[pl.BlockSpec((CHIPS, rows, step), lambda n, place: (0, 0, n))] * 2,
        ),
        out_shape=(out, out),
        compiler_params=space(8),
        name="project",
    )(place, attn, weight)


def pair_kernel(mine, other, *outs):
    for i in range(CHIPS):
        outs[i][...] = (mine[i].astype(f32) + other[i].astype(f32)).astype(bf16)


def pair_sums(mine, other):
    out = jax.ShapeDtypeStruct(mine.shape[1:], bf16)
    return pl.pallas_call(
        pair_kernel, out_shape=(out,) * CHIPS, compiler_params=space(6), name="pair_sums"
    )(mine, other)


def front_kernel(place, p0, p1, p2, p3, residual, gain, router, shares0, shares1, _, *outs):
    outbox0, outbox1, stream_out, logits_out = outs
    rows = p0.shape[0]
    start = (2 * place[0] + place[1]) * rows
    total = (p0[...].astype(f32) + p1[...].astype(f32)) + (
        p2[...].astype(f32) + p3[...].astype(f32)
    )
    mine = residual[pl.ds(pl.multiple_of(start, rows), rows), :]
    stream = (mine.astype(f32) + total).astype(bf16)
    wide = stream.astype(f32)
    scale = lax.rsqrt(jnp.mean(wide * wide, axis=-1, keepdims=True) + epsilon)
    normed = (wide * scale * gain[...]).astype(bf16)
    stream_out[...] = pieces_to_rows(stream)
    logits_out[...] = dot_last(normed, router[...])
    by_piece = pieces_to_rows(normed)
    for shares, outbox in ((shares0, outbox0), (shares1, outbox1)):
        hits = (shares[...] != 0.0).astype(bf16)
        outbox[...] = dot_first(hits, by_piece).astype(bf16)


def front(place, parts, residual, gain, router, shares, after):
    rows, width = parts[0].shape
    piece = width // PIECES
    whole = pl.BlockSpec(memory_space=pltpu.VMEM)
    outbox = jax.ShapeDtypeStruct((shares[0].shape[1], piece), bf16)
    return pl.pallas_call(
        front_kernel,
        in_specs=[pl.BlockSpec(memory_space=pltpu.SMEM)]
        + [whole] * 9
        + [pl.BlockSpec(memory_space=pl.ANY)],
        out_shape=(
            outbox,
            outbox,
            jax.ShapeDtypeStruct((rows * PIECES, piece), bf16),
            jax.ShapeDtypeStruct((rows, router.shape[0]), f32),
        ),
        compiler_params=space(10),
        name="front",
    )(place, *parts, residual, gain, router, *shares, after)


def by_piece_kernel(x, order, out):
    moved = jnp.dot(order[...], x[...], preferred_element_type=f32)
    out[...] = moved.reshape(out.shape).astype(bf16)


def rows_by_piece(x, order):
    size = order.shape[0]
    steps = x.shape[0] // size
    width = x.shape[1]
    run = size // PIECES
    return pl.pallas_call(
        by_piece_kernel,
        grid=(steps,),
        in_specs=[
            pl.BlockSpec((size, width), lambda a: (a, 0)),
            pl.BlockSpec((size, size), lambda a: (0, 0)),
        ],
        out_specs=pl.BlockSpec((PIECES, run, width), lambda a: (0, a, 0)),
        out_shape=jax.ShapeDtypeStruct((PIECES, run * steps, width), bf16),
        compiler_params=space(6),
        name="rows_by_piece",
    )(x, order)


def up_kernel(r0, r1, r2, r3, gate_own, gate_other, up_own, up_other, *refs):
    *outs, gate, up = refs
    step = pl.program_id(0)
    width = r0.shape[2]

    @pl.when(step == 0)
    def _():
        gate[...] = jnp.zeros_like(gate)
        up[...] = jnp.zeros_like(up)

    for q in range(r0.shape[0]):
        x = jnp.concatenate([r0[q], r1[q], r2[q], r3[q]], axis=0)
        at = slice(q * width, (q + 1) * width)
        gate[...] += dot_last(x, jnp.concatenate([gate_own[:, at], gate_other[:, at]], axis=0))
        up[...] += dot_last(x, jnp.concatenate([up_own[:, at], up_other[:, at]], axis=0))

    @pl.when(step == pl.num_programs(0) - 1)
    def _():
        g = gate[...]
        hidden = (g / (1.0 + jnp.exp(-g)) * up[...]).astype(bf16)
        rows = outs[0].shape[0]
        for i in range(CHIPS):
            outs[i][...] = hidden[i * rows : (i + 1) * rows, :]


def up_rows(sources, weights):
    pieces, rows, width = sources[0].shape
    half = pieces // 2
    units = weights[0].shape[0]
    out = jax.ShapeDtypeStruct((rows, 2 * units), bf16)
    return pl.pallas_call(
        up_kernel,
        grid=(2,),
        in_specs=[pl.BlockSpec((half, rows, width), lambda j: (j, 0, 0))] * CHIPS
        + [pl.BlockSpec((units, half * width), lambda j: (0, j))] * 4,
        out_specs=[pl.BlockSpec((rows, 2 * units), lambda j: (0, 0))] * CHIPS,
        out_shape=(out,) * CHIPS,
        scratch_shapes=[pltpu.VMEM((CHIPS * rows, 2 * units), f32)] * 2,
        compiler_params=space(15),
        name="up_rows",
    )(*sources, *weights)


def down_kernel(*refs):
    hidden, refs = refs[:CHIPS], refs[CHIPS:]
    weights, (order, out, held) = refs[: 2 * CHIPS], refs[2 * CHIPS :]
    step = pl.program_id(0)
    total = None
    for i in range(CHIPS):
        weight = jnp.concatenate([weights[2 * i][...], weights[2 * i + 1][...]], axis=0)
        part = jnp.dot(hidden[i][...], weight, preferred_element_type=f32)
        total = part if total is None else total + part
    total = total.astype(bf16)
    width = held.shape[2]
    count = total.shape[1] // width
    for q in range(count):
        held[step * count + q] = total[:, q * width : (q + 1) * width]

    @pl.when(step == pl.num_programs(0) - 1)
    def _():
        size = order.shape[0]
        run = size // PIECES
        for a in range(held.shape[1] // run):
            block = held[:, a * run : (a + 1) * run, :].reshape(size, width)
            out[a * size : (a + 1) * size, :] = dot_first(order[...], block).astype(bf16)


def down_rows(hidden, weights, order):
    rows, units = hidden[0].shape
    depth, width = weights[0].shape
    piece = width // PIECES
    steps = 4
    return pl.pallas_call(
        down_kernel,
        grid=(steps,),
        in_specs=[pl.BlockSpec((rows, units), lambda j: (0, 0))] * CHIPS
        + [pl.BlockSpec((depth, width // steps), lambda j: (0, j))] * (2 * CHIPS)
        + [pl.BlockSpec(order.shape, lambda j: (0, 0))],
        out_specs=pl.BlockSpec((rows * PIECES, piece), lambda j: (0, 0)),
        out_shape=jax.ShapeDtypeStruct((rows * PIECES, piece), bf16),
        scratch_shapes=[pltpu.VMEM((PIECES, rows, piece), bf16)],
        compiler_params=space(11),
        name="down_rows",
    )(*hidden, *weights, order)


def finish_kernel(back0, back1, weights0, weights1, stream, logits, out):
    moe = stream[...].astype(f32)
    for back, weights in ((back0, weights0), (back1, weights1)):
        high = weights[...].astype(bf16)
        low = (weights[...] - high.astype(f32)).astype(bf16)
        moe = moe + (
            jnp.dot(high, back[...], preferred_element_type=f32)
            + jnp.dot(low, back[...], preferred_element_type=f32)
        )
    rows = stream.shape[0]
    out[0:rows, :] = moe.astype(bf16)
    logit_high = logits[...].astype(bf16)
    logit_low = (logits[...] - logit_high.astype(f32)).astype(bf16)
    filler = jnp.zeros((logits.shape[0], out.shape[1] - 2 * logits.shape[1]), bf16)
    out[rows:, :] = jnp.concatenate([logit_high, logit_low, filler], axis=1)


def finish(returned, weights, stream, logits):
    return pl.pallas_call(
        finish_kernel,
        out_shape=jax.ShapeDtypeStruct(
            (stream.shape[0] + logits.shape[0], stream.shape[1]), bf16
        ),
        compiler_params=space(6),
        name="finish",
    )(*returned, *weights, stream, logits)


def assemble_kernel(place, same_core, other_core, mixed, logits):
    rows = mixed.shape[0] // (2 * CHIPS)
    piece = same_core.shape[2]
    count = logits.shape[1]
    for other, blocks in enumerate((same_core, other_core)):
        for shift in range(CHIPS):
            rank = 2 * ((place[0] + CHIPS - shift) % CHIPS) + (place[1] + other) % 2
            at = pl.ds(pl.multiple_of(rank * rows, rows), rows)
            for j in range(PIECES):
                mixed[at, j * piece : (j + 1) * piece] = blocks[
                    shift, j * rows : (j + 1) * rows, :
                ]
            tail = blocks[shift, PIECES * rows :, :].astype(f32)
            logits[at, :] = tail[:, :count] + tail[:, count : 2 * count]


def assemble(place, same_core, other_core, expert_count):
    rows = same_core.shape[1] // (PIECES + 1)
    width = same_core.shape[2] * PIECES
    whole = pl.BlockSpec(memory_space=pltpu.VMEM)
    return pl.pallas_call(
        assemble_kernel,
        in_specs=[pl.BlockSpec(memory_space=pltpu.SMEM), whole, whole],
        out_shape=(
            jax.ShapeDtypeStruct((rows * 2 * CHIPS, width), bf16),
            jax.ShapeDtypeStruct((rows * 2 * CHIPS, expert_count), f32),
        ),
        compiler_params=space(6),
        name="assemble",
    )(place, same_core, other_core)


def routing(chosen, combine, expert_count, capacity):
    targets = slot_targets(chosen, expert_count, capacity)
    tokens = chosen.shape[0]
    slots = capacity // HALVES
    run = PIECES * slots
    total = expert_count * run
    row = lax.broadcasted_iota(jnp.int32, (PIECES * tokens, total), 0)
    col = lax.broadcasted_iota(jnp.int32, (PIECES * tokens, total), 1)
    same_piece = row // tokens == (col % run) // slots
    targets = jnp.tile(targets, (PIECES, 1))
    combine = jnp.tile(combine, (PIECES, 1))
    results = []
    for half in range(HALVES):
        slot_of = col // run * capacity + half * slots + col % slots
        wanted = jnp.where(same_piece, slot_of, -1)
        weights = jnp.zeros((PIECES * tokens, total), f32)
        for k in range(chosen.shape[1]):
            weights = jnp.where(wanted == targets[:, k : k + 1], combine[:, k : k + 1], weights)
        results.append(weights)
    return results


def shards(
    attn_out,
    residual,
    o_weight,
    norm_gain,
    router_weight,
    expert_idx,
    combine,
    w_gate,
    w_up,
    w_down,
):
    ranks = lax.axis_size("tensor")
    rank = lax.axis_index("tensor")
    place = jnp.stack([rank // 2, rank % 2]).astype(jnp.int32)
    group_rows, width = residual.shape
    rows = group_rows // ranks
    expert_count = router_weight.shape[1]
    top_count = expert_idx.shape[1]
    capacity = min(rows, max(2, 3 * rows * top_count // (2 * expert_count)))
    slots = capacity // HALVES

    down_next, down_last = around(w_down[0], 1), around(w_down[0], -1)
    down_far = around(down_next, 1)
    gate_own, up_own = w_gate[0].T, w_up[0].T
    weights = (gate_own, across(gate_own), up_own, across(up_own))
    order = reorder_matrix(PIECES, BATCH, slots)
    chosen = lax.dynamic_slice_in_dim(expert_idx, rank * rows, rows, 0)
    my_combine = lax.dynamic_slice_in_dim(combine, rank * rows, rows, 0)
    shares = routing(chosen, my_combine, expert_count, capacity)

    mine, theirs = project(place, attn_out, o_weight)
    sums = pair_sums(mine, across(theirs))
    parts = (sums[0],) + tuple(along(sums[shift], shift) for shift in range(1, CHIPS))
    other_own, other_next, other_last = (across(w_down[0]), across(down_last), across(down_next))
    other_far = across(down_far)
    down_weights = [
        w_down[0],
        other_own,
        down_next,
        other_next,
        down_far,
        other_far,
        down_last,
        other_last,
    ]
    outbox0, outbox1, stream, logits = front(
        place, parts, residual, norm_gain.reshape(1, width), router_weight.T, shares, order
    )
    arrived = []
    for outbox in (outbox0, outbox1):
        arrived.append(lax.all_to_all(outbox, "expert", split_axis=0, concat_axis=0, tiled=True))
    own = []
    for x in arrived:
        own.append(rows_by_piece(x, order))
    returned = []
    for mine in own:
        following = around(mine, 1)
        last = around(mine, -1)
        far = around(following, 1)
        hidden = up_rows((mine, following, far, last), weights)
        units = (
            hidden[0],
            around(hidden[3], 1),
            along(hidden[2], 2),
            around(hidden[1], -1),
        )
        expert_out = down_rows(units, down_weights, order)
        returned.append(
            lax.all_to_all(expert_out, "expert", split_axis=0, concat_axis=0, tiled=True)
        )
    packed = finish(returned, shares, stream, logits)
    same_core = jnp.stack([packed] + [along(packed, shift) for shift in range(1, CHIPS)])
    return assemble(place, same_core, across(same_core), expert_count)


def solution(mesh):
    in_specs = (
        P("expert", "tensor"),
        P("expert", None),
        P("tensor", None),
        P(),
        P(),
        P("expert", None),
        P("expert", None),
        P("expert", None, "tensor"),
        P("expert", None, "tensor"),
        P("expert", "tensor", None),
    )
    out_specs = (P("expert", None), P("expert", None))

    return jax.shard_map(shards, mesh=mesh, in_specs=in_specs, out_specs=out_specs, check_vma=False)
```
